256 devices in a mesh: row: 16 (over z_hi, x), col: 16 (over z_lo, y, core).
Axes of the slice: x: 4, y: 4, z: 8 (z_hi: 4, z_lo: 2; z = z_hi * 2 + z_lo), core: 2. Of those that a mesh axis runs over, the one named last changes fastest.
Arguments:
- features: bfloat16 [32768, 1024], P(('col', 'row')), may hold values from -6 to 6
- weight: bfloat16 [1024, 1024], P('col'), may hold values from -0.1875 to 0.1875
- tile_values: bfloat16 [16, 16, 16, 8, 128, 128], P('row', 'col'), may hold values from -0.0625 to 0.0625
- block_cols: int32 [16, 16, 16, 8], P('row', 'col'), may hold values from 0 to 15, as said below
- tile_counts: int32 [16, 16, 16], P('row', 'col'), may hold values from 1 to 8, as said below
Outputs:
- hidden_out: bfloat16 [32768, 1024], P(('row', 'col'))
The draws below stay inside these ranges and needn't reach their ends.
Inputs may be any that keep to these rules, and one draw needn't show every extreme that they name: `block_cols`: the 8 entries of one block row of a tile are distinct block columns; values and block columns of slots that are not live are arbitrary. `tile_counts`: every tile has a block row with all 8 slots live.
All inputs are finite; a program needn't handle non-finite values.
Results may differ from the reference program's by a relative error of at most 0.019.
Values may be sent and summed in bfloat16 or wider, within the bound.
No kernel may reach another device: no remote copies, remote signals or barrier semaphores. Data moves between devices by JAX's collectives and lax.ppermute only.
A program may use at most 64 MiB of HBM per device.

```python
import jax
import jax.numpy as jnp
from jax import lax

FEAT = 1024
BS = 128
SLOTS = 8
ROW_BLK = 16
COL_BLK = 16
NODES = 32768
N_ROW = 16
N_COL = 16


def draw_block_cols(key, part):
    scores = jax.random.randint(key, (N_ROW, N_COL, ROW_BLK, COL_BLK), 0, 2 ** 20, dtype=jnp.int32)
    scores = scores * COL_BLK + jnp.arange(COL_BLK, dtype=jnp.int32)
    order = jnp.argsort(scores, axis=-1, stable=True)
    return order[..., :SLOTS].astype(jnp.int32)


def draw_tile_counts(key, part):
    base_key = jax.random.fold_in(key, 11)
    floor_key = jax.random.fold_in(key, 23)
    where_key = jax.random.fold_in(key, 37)
    base = jax.random.randint(base_key, (N_ROW, N_COL, ROW_BLK), 1, SLOTS + 1, dtype=jnp.int32)
    floor_level = jax.random.randint(floor_key, (N_ROW, N_COL, 1), 1, SLOTS + 1, dtype=jnp.int32)
    counts = jnp.maximum(base, floor_level)
    full_row = jax.random.randint(where_key, (N_ROW, N_COL, 1), 0, ROW_BLK, dtype=jnp.int32)
    positions = jnp.arange(ROW_BLK, dtype=jnp.int32)[None, None, :]
    return jnp.where(positions == full_row, SLOTS, counts).astype(jnp.int32)


def shard_levels(rng, dims, cuts, least, high):
    level, own = 1.0, jax.random.fold_in(rng, 6)
    for position, shards_of in cuts:
        draws = jnp.exp(jax.random.uniform(jax.random.fold_in(own, position), (shards_of,), jnp.float32, least / len(cuts), high / len(cuts)))
        level = level * jnp.repeat(draws, dims[position] // shards_of).reshape([-1 if axis == position else 1 for axis in range(len(dims))])
    return level


def noise(own_key, extent, deviation, most, pieces=(), kind=jnp.bfloat16):
    array = deviation * jax.random.normal(own_key, extent, jnp.float32)
    if pieces:
        array = array * shard_levels(own_key, extent, pieces, -0.22, 0.18)
    return jnp.clip(array, -most, most).astype(kind)


def setup_inputs(seed: int = 0) -> dict:
    streams_of = jax.random.split(jax.random.key(seed), 6)
    features = noise(streams_of[0], (NODES, FEAT), 1.0, 6.0, ((0, 256),))
    weight = noise(streams_of[1], (FEAT, FEAT), FEAT ** -0.5, 0.1875, ((0, 16),))
    tile_values = noise(streams_of[2], (N_ROW, N_COL, ROW_BLK, SLOTS, BS, BS), (BS * SLOTS * N_COL // 2) ** -0.5, 0.0625, ((0, 16), (1, 16)))
    block_cols = draw_block_cols(jax.random.fold_in(streams_of[5], 71), 0)
    tile_counts = draw_tile_counts(jax.random.fold_in(streams_of[5], 71), 0)
    return {"features": features, "weight": weight, "tile_values": tile_values, "block_cols": block_cols, "tile_counts": tile_counts}


def tile_term(slot_values, slot_cols, slot_count, column_rows):
    slot_total = slot_values.shape[1]
    block_size = slot_values.shape[-1]
    by_block = column_rows.reshape(-1, block_size, column_rows.shape[-1])
    gathered = by_block[slot_cols]
    live_slots = jnp.arange(slot_total, dtype=jnp.int32)[None, :] < slot_count[:, None]
    masked = jnp.where(live_slots[:, :, None, None], slot_values, jnp.zeros_like(slot_values))
    product = jnp.einsum('rsab,rsbf->raf', masked.astype(jnp.float32), gathered.astype(jnp.float32))
    return product.reshape(-1, product.shape[-1])


def reference(features, weight, tile_values, block_cols, tile_counts):
    panel_rows = COL_BLK * BS

    def one_panel(row_args):
        values_row, cols_row, counts_row = row_args

        def add_tile(running, tile_args):
            values_tile, cols_tile, counts_tile, column = tile_args
            column_rows = lax.dynamic_slice_in_dim(features, column * panel_rows, panel_rows, 0)
            rounded = tile_term(values_tile, cols_tile, counts_tile, column_rows).astype(jnp.bfloat16)
            rounded = lax.optimization_barrier(rounded)
            return running + rounded.astype(jnp.float32), None

        start_sum = jnp.zeros((ROW_BLK * BS, FEAT), jnp.float32)
        columns = jnp.arange(N_COL, dtype=jnp.int32)
        summed, unused = lax.scan(add_tile, start_sum, (values_row, cols_row, counts_row, columns))
        return summed.astype(jnp.bfloat16)

    aggregated = lax.map(one_panel, (tile_values, block_cols, tile_counts)).reshape(NODES, FEAT)
    product = jnp.dot(aggregated, weight, preferred_element_type=jnp.float32)
    return jnp.maximum(product, 0.0).astype(jnp.bfloat16)
```

```python
import functools

import jax
import jax.numpy as jnp
from jax import lax
from jax.experimental import pallas as pl
from jax.experimental.pallas import tpu as pltpu
from jax.sharding import PartitionSpec as P


BS = 128
K_ORDER = (
    (0, 0), (0, 3), (0, 1), (0, 2),
    (3, 0), (1, 0), (2, 0), (3, 3), (3, 1), (1, 3), (1, 1), (3, 2),
    (1, 2), (2, 3), (2, 1), (2, 2),
)
ROW_ORDER = (
    (1, 0, 2), (1, 1, 2),
    (1, 0, 3), (1, 1, 3), (1, 0, 1), (1, 1, 1),
    (0, 0, 2), (0, 1, 2),
    (1, 0, 0), (1, 1, 0),
    (0, 0, 3), (0, 1, 3), (0, 0, 1), (0, 1, 1),
    (0, 0, 0), (0, 1, 0),
)
VMEM = 24 << 20


def moves():
    every = [(zh, x, zl, y, c) for zh in range(4) for x in range(4) for zl in range(2) for y in range(4) for c in range(2)]

    def flat(zh, x, zl, y, c):
        return ((zh % 4) * 4 + x % 4) * 16 + (zl % 2) * 8 + (y % 4) * 2 + c % 2

    def table(shift):
        return [(flat(*p), flat(*shift(*p, 1 - 2 * p[4]))) for p in every]

    return {
        "fx": table(lambda zh, x, zl, y, c, s: (zh, x + s, zl, y, c)),
        "gx": table(lambda zh, x, zl, y, c, s: (zh, x - s, zl, y, c)),
        "fz": table(lambda zh, x, zl, y, c, s: (zh + s, x, zl, y, c)),
        "gz": table(lambda zh, x, zl, y, c, s: (zh - s, x, zl, y, c)),
        "fy": table(lambda zh, x, zl, y, c, s: (zh, x, zl, y + s, c)),
        "gy": table(lambda zh, x, zl, y, c, s: (zh, x, zl, y - s, c)),
        "zl": table(lambda zh, x, zl, y, c, s: (zh, x, zl + 1, y, c)),
        "core": table(lambda zh, x, zl, y, c, s: (zh, x, zl, y, c + 1)),
    }


def dense_kernel(tab, cols, counts, values_ref, out_ref):
    q = pl.program_id(0)
    r = tab[q]
    z, x, sign = tab[32], tab[33], tab[34]
    out_ref[...] = jnp.zeros_like(out_ref)
    for s in range(8):
        @pl.when(s < counts[r])
        def _():
            b = cols[r * 8 + s]
            sz = (sign * ((b >> 2) - z)) & 3
            sx = (sign * ((b & 3) - x)) & 3
            at = pl.multiple_of(tab[16 + sz * 4 + sx] * BS, BS)
            out_ref[:, pl.ds(at, BS)] = values_ref[0, s]


def dense_tile(tab, cols, counts, values):
    return pl.pallas_call(
        dense_kernel,
        out_shape=jax.ShapeDtypeStruct((2048, 2048), jnp.bfloat16),
        grid_spec=pltpu.PrefetchScalarGridSpec(
            num_scalar_prefetch=3,
            grid=(16,),
            in_specs=[pl.BlockSpec((1, 8, BS, BS), lambda q, tab, cols, counts: (tab[q], 0, 0, 0))],
            out_specs=pl.BlockSpec((BS, 2048), lambda q, tab, cols, counts: (q, 0)),
        ),
        compiler_params=pltpu.CompilerParams(vmem_limit_bytes=VMEM),
        cost_estimate=pl.CostEstimate(flops=0, transcendentals=0, bytes_accessed=12 << 20),
        name="dense_tile",
    )(tab, cols, counts, values)


def mm_kernel(nb, has_acc, has_add, a_ref, *refs):
    blocks, rest = refs[:nb], list(refs[nb:])
    acc_ref = rest.pop(0) if has_acc else None
    add_ref = rest.pop(0) if has_add else None
    out_ref, joined = rest

    @pl.when(pl.program_id(0) == 0)
    def _():
        for k, block in enumerate(blocks):
            joined[k * BS:(k + 1) * BS, :] = block[...]

    total = jnp.dot(a_ref[...], joined[...], preferred_element_type=jnp.float32)
    if has_acc:
        total = total + acc_ref[...]
    if has_add:
        total = total + add_ref[...].astype(jnp.float32)
    out_ref[...] = total.astype(out_ref.dtype)


def mm(name, dense, first_k, blocks, rows, acc=None, add=None, dtype=jnp.bfloat16, tm=256):
    nb, depth = len(blocks), len(blocks) * BS
    start, count = rows[0] * BS // tm, rows[1] * BS // tm
    whole = pl.BlockSpec((BS, 1024), lambda i: (0, 0))
    k_block = first_k * BS // depth
    assert k_block * depth == first_k * BS and start * tm == rows[0] * BS
    specs = [pl.BlockSpec((tm, depth), lambda i: (start + i, k_block))] + [whole] * nb
    args = [dense, *blocks]
    if acc is not None:
        specs.append(pl.BlockSpec((tm, 1024), lambda i: (start + i, 0)))
        args.append(acc)
    if add is not None:
        array, offset = add
        first = offset * BS // tm
        specs.append(pl.BlockSpec((tm, 1024), lambda i: (first + i, 0)))
        args.append(array)
    return pl.pallas_call(
        functools.partial(mm_kernel, nb, acc is not None, add is not None),
        out_shape=jax.ShapeDtypeStruct((count * tm, 1024), dtype),
        grid_spec=pltpu.PrefetchScalarGridSpec(
            num_scalar_prefetch=0,
            grid=(count,),
            in_specs=specs,
            out_specs=pl.BlockSpec((tm, 1024), lambda i: (i, 0)),
            scratch_shapes=[pltpu.VMEM((depth, 1024), jnp.bfloat16)],
        ),
        compiler_params=pltpu.CompilerParams(vmem_limit_bytes=VMEM),
        cost_estimate=pl.CostEstimate(
            flops=2 * count * tm * depth * 1024, transcendentals=0,
            bytes_accessed=count * tm * (depth * 2 + 1024 * 8) + depth * 2048),
        name=name,
    )(*args)


def join_weight_kernel(tab, mine_ref, other_ref, out_ref):
    for half, ref in enumerate((mine_ref, other_ref)):
        for k in range(8):
            at = pl.multiple_of(tab[36 + half * 8 + k] * 64, 64)
            out_ref[pl.ds(at, 64), :] = ref[k * 64:(k + 1) * 64, :]


def join_weight(tab, mine, other):
    return pl.pallas_call(
        join_weight_kernel,
        out_shape=jax.ShapeDtypeStruct((1024, 1024), jnp.bfloat16),
        grid_spec=pltpu.PrefetchScalarGridSpec(
            num_scalar_prefetch=1,
            grid=(1,),
            in_specs=[pl.BlockSpec((512, 1024), lambda i, tab: (0, 0))] * 2,
            out_specs=pl.BlockSpec((1024, 1024), lambda i, tab: (0, 0)),
        ),
        compiler_params=pltpu.CompilerParams(vmem_limit_bytes=VMEM),
        cost_estimate=pl.CostEstimate(flops=0, transcendentals=0, bytes_accessed=4 << 20),
        name="join_weight",
    )(tab, mine, other)


def last_kernel(a_ref, b_ref, c_ref, d_ref, w_ref, out_ref):
    total = a_ref[...].astype(jnp.float32) + b_ref[...].astype(jnp.float32)
    total = total + c_ref[...].astype(jnp.float32) + d_ref[...].astype(jnp.float32)
    product = jnp.dot(total.astype(jnp.bfloat16), w_ref[...], preferred_element_type=jnp.float32)
    out_ref[...] = jnp.maximum(product, 0.0).astype(out_ref.dtype)


def last(s0, f0, g0, far, weight):
    block = pl.BlockSpec((BS, 1024), lambda n: (0, 0))
    return pl.pallas_call(
        last_kernel,
        out_shape=jax.ShapeDtypeStruct((BS, 1024), jnp.bfloat16),
        grid=(1,),
        in_specs=[block, block, block, block, pl.BlockSpec((1024, 1024), lambda n: (0, 0))],
        out_specs=pl.BlockSpec((BS, 1024), lambda n: (0, 0)),
        compiler_params=pltpu.CompilerParams(vmem_limit_bytes=VMEM),
        cost_estimate=pl.CostEstimate(flops=2 * BS * 1024 * 1024, transcendentals=0, bytes_accessed=3 << 20),
        name="last",
    )(s0, f0, g0, far, weight)


def add32(*terms):
    total = terms[0].astype(jnp.float32)
    for term in terms[1:]:
        total = total + term.astype(jnp.float32)
    return total.astype(jnp.bfloat16)


def body(features, weight, tile_values, block_cols, tile_counts):
    perms = moves()

    def go(move, x):
        with jax.named_scope("go_" + move):
            return lax.ppermute(x, ("row", "col"), perms[move])

    row, col = lax.axis_index("row"), lax.axis_index("col")
    z, x = row // 4, row % 4
    zl, y, core = col // 8, (col // 2) % 4, col % 2
    sign = 1 - 2 * core

    send, dz, dy = (jnp.array(v, jnp.int32) for v in zip(*ROW_ORDER))
    owner_y = (y + sign * (1 - 2 * send) * dy) & 3
    owner = (zl ^ dz) * 8 + owner_y * 2 + (core ^ send)
    where = [0] * 16
    for k, (sz, sx) in enumerate(K_ORDER):
        where[sz * 4 + sx] = k
    w_dy = jnp.array([0, 0, 3, 3, 1, 1, 2, 2] * 2, jnp.int32)
    w_dz = jnp.array([0, 1] * 8, jnp.int32)
    w_other = jnp.array([0] * 8 + [1] * 8, jnp.int32)
    w_at = (zl ^ w_dz) * 8 + ((y + sign * (1 - 2 * w_other) * w_dy) & 3) * 2 + (core ^ w_other)
    misc = jnp.stack([z, x, sign, core]).astype(jnp.int32)
    tab = jnp.concatenate([owner.astype(jnp.int32), jnp.array(where, jnp.int32), misc, w_at.astype(jnp.int32)])

    b = {(0, 0): features}
    b[0, 3], b[0, 1] = go("fx", features), go("gx", features)
    b[3, 0], b[1, 0] = go("fz", features), go("gz", features)
    b[0, 2] = go("fx", b[0, 3])
    b[2, 0] = go("fz", b[3, 0])
    b[3, 3], b[3, 1] = go("fx", b[3, 0]), go("gx", b[3, 0])
    b[1, 3], b[1, 1] = go("fx", b[1, 0]), go("gx", b[1, 0])
    b[3, 2], b[1, 2] = go("fz", b[0, 2]), go("gz", b[0, 2])
    b[2, 3], b[2, 1] = go("fx", b[2, 0]), go("gx", b[2, 0])
    b[2, 2] = go("fx", b[2, 3])
    in_order = [b[key] for key in K_ORDER]

    w2 = jnp.concatenate([weight, go("zl", weight)], axis=0)
    w3, w1 = go("fy", w2), go("gy", w2)
    w_mine = jnp.concatenate([w2, w3, w1, go("fy", w3)], axis=0)
    w_full = join_weight(tab, w_mine, go("core", w_mine))

    dense = dense_tile(tab, block_cols.reshape(128), tile_counts.reshape(16), tile_values[0, 0])
    acc = mm("mm_a", dense, 0, in_order[:4], (0, 16), dtype=jnp.float32)
    acc = mm("mm_b", dense, 4, in_order[4:8], (0, 16), acc=acc, dtype=jnp.float32)
    acc = mm("mm_c", dense, 8, in_order[8:12], (0, 16), acc=acc, dtype=jnp.float32)
    tail = in_order[12:]

    def rows(name, start, count, add=None):
        return mm(name, dense, 12, tail, (start, count), acc=acc, add=add)

    send2 = rows("send2", 0, 2)
    got2 = go("core", send2)
    send31 = rows("send31", 2, 4)
    got31 = go("core", send31)
    s2 = rows("keep2", 6, 2, (got2, 0))
    from2 = go("fy", s2)
    send0 = rows("send0", 8, 2)
    got0 = go("core", send0)
    s3 = rows("keep3", 10, 2, (got31, 0))
    g0 = go("gy", s3)
    s1 = rows("keep1", 12, 2, (got31, 2))
    s0 = rows("keep0", 14, 2, (got0, 0))
    f0_far = go("fy", add32(s1[BS:], from2[BS:]))
    f0_near = go("fy", add32(s1[:BS], from2[:BS]))
    far = go("zl", add32(s0[BS:], g0[BS:], f0_far))
    return last(s0[:BS], g0[:BS], f0_near, far, w_full)


def solution(mesh):
    in_specs = (
        P(("col", "row"), None),
        P("col", None),
        P("row", "col", None, None, None, None),
        P("row", "col", None, None),
        P("row", "col", None),
    )
    out_specs = P(("row", "col"), None)
    return jax.shard_map(body, mesh=mesh, in_specs=in_specs, out_specs=out_specs, check_vma=False)
```

```python
import functools

import jax
import jax.numpy as jnp
from jax import lax
from jax.experimental import pallas as pl
from jax.experimental.pallas import tpu as pltpu
from jax.sharding import PartitionSpec as P


BS = 128
K_ORDER = (
    (0, 0), (0, 3), (0, 1), (0, 2),
    (3, 0), (1, 0), (2, 0), (3, 3), (3, 1), (1, 3), (1, 1), (3, 2),
    (1, 2), (2, 3), (2, 1), (2, 2),
)
ROW_ORDER = (
    (1, 0, 2), (1, 1, 2),
    (1, 0, 3), (1, 1, 3), (1, 0, 1), (1, 1, 1),
    (0, 0, 2), (0, 1, 2),
    (1, 0, 0), (1, 1, 0),
    (0, 0, 3), (0, 1, 3), (0, 0, 1), (0, 1, 1),
    (0, 0, 0), (0, 1, 0),
)
VMEM = 13 << 20


def moves():
    every = [(zh, x, zl, y, c) for zh in range(4) for x in range(4) for zl in range(2) for y in range(4) for c in range(2)]

    def flat(zh, x, zl, y, c):
        return ((zh % 4) * 4 + x % 4) * 16 + (zl % 2) * 8 + (y % 4) * 2 + c % 2

    def table(shift):
        return [(flat(*p), flat(*shift(*p, 1 - 2 * p[4]))) for p in every]

    return {
        "fx": table(lambda zh, x, zl, y, c, s: (zh, x + s, zl, y, c)),
        "gx": table(lambda zh, x, zl, y, c, s: (zh, x - s, zl, y, c)),
        "fz": table(lambda zh, x, zl, y, c, s: (zh + s, x, zl, y, c)),
        "gz": table(lambda zh, x, zl, y, c, s: (zh - s, x, zl, y, c)),
        "fy": table(lambda zh, x, zl, y, c, s: (zh, x, zl, y + s, c)),
        "gy": table(lambda zh, x, zl, y, c, s: (zh, x, zl, y - s, c)),
        "zl": table(lambda zh, x, zl, y, c, s: (zh, x, zl + 1, y, c)),
        "core": table(lambda zh, x, zl, y, c, s: (zh, x, zl, y, c + 1)),
    }


def place(pos):
    row, col = pos[0], pos[1]
    core = col & 1
    return row >> 2, row & 3, col >> 3, (col >> 1) & 3, core, 1 - 2 * core


def pack(values, bits):
    per = 32 // bits
    words = []
    for first in range(0, len(values), per):
        word = sum(v << (bits * k) for k, v in enumerate(values[first:first + per]))
        words.append(word - (1 << 32) if word >= 1 << 31 else word)
    return words


K_AT = [K_ORDER.index((k >> 2, k & 3)) for k in range(16)]
K_LOW, K_HIGH = pack(K_AT, 4)
(ROW_WORD,), (DZ_WORD,), (DY_WORD,) = (pack(v, 2 if n == 2 else 1) for n, v in enumerate(zip(*ROW_ORDER)))


def row_owner(q, pos):
    _, _, zl, y, core, sign = place(pos)
    sent = (jnp.int32(ROW_WORD) >> q) & 1
    dz = (jnp.int32(DZ_WORD) >> q) & 1
    dy = (jnp.int32(DY_WORD) >> (2 * q)) & 3
    return (zl ^ dz) * 8 + ((y + sign * (1 - 2 * sent) * dy) & 3) * 2 + (core ^ sent)


def dense_kernel(pos, cols, counts, values_ref, out_ref):
    r = row_owner(pl.program_id(0), pos)
    z, x, _, _, _, sign = place(pos)
    out_ref[...] = jnp.zeros_like(out_ref)
    for s in range(8):
        @pl.when(s < counts[r])
        def _():
            b = cols[r * 8 + s]
            key = (((sign * ((b >> 2) - z)) & 3) << 2) | ((sign * ((b & 3) - x)) & 3)
            word = jnp.where(key < 8, jnp.int32(K_LOW), jnp.int32(K_HIGH))
            at = pl.multiple_of(((word >> ((key & 7) * 4)) & 15) * BS, BS)
            out_ref[:, pl.ds(at, BS)] = values_ref[0, s]


def dense_tile(pos, cols, counts, values):
    return pl.pallas_call(
        dense_kernel,
        out_shape=jax.ShapeDtypeStruct((2048, 2048), jnp.bfloat16),
        grid_spec=pltpu.PrefetchScalarGridSpec(
            num_scalar_prefetch=3,
            grid=(16,),
            in_specs=[pl.BlockSpec((1, 8, BS, BS), lambda q, pos, cols, counts: (row_owner(q, pos), 0, 0, 0))],
            out_specs=pl.BlockSpec((BS, 2048), lambda q, pos, cols, counts: (q, 0)),
        ),
        compiler_params=pltpu.CompilerParams(vmem_limit_bytes=VMEM),
        cost_estimate=pl.CostEstimate(flops=0, transcendentals=0, bytes_accessed=12 << 20),
        name="dense_tile",
    )(pos, cols, counts, values)


def mm_kernel(nb, has_acc, has_add, a_ref, *refs):
    blocks, rest = refs[:nb], list(refs[nb:])
    acc_ref = rest.pop(0) if has_acc else None
    add_ref = rest.pop(0) if has_add else None
    out_ref, joined = rest

    @pl.when(pl.program_id(0) == 0)
    def _():
        for k, block in enumerate(blocks):
            joined[k * BS:(k + 1) * BS, :] = block[...]

    total = jnp.dot(a_ref[...], joined[...], preferred_element_type=jnp.float32)
    if has_acc:
        total = total + acc_ref[...]
    if has_add:
        total = total + add_ref[...].astype(jnp.float32)
    out_ref[...] = total.astype(out_ref.dtype)


def mm(dense, first_k, blocks, rows, acc=None, add=None, dtype=jnp.bfloat16, tm=256):
    nb, depth = len(blocks), len(blocks) * BS
    start, count = rows[0] * BS // tm, rows[1] * BS // tm
    whole = pl.BlockSpec((BS, 1024), lambda i: (0, 0))
    k_block = first_k * BS // depth
    assert k_block * depth == first_k * BS and start * tm == rows[0] * BS
    specs = [pl.BlockSpec((tm, depth), lambda i: (start + i, k_block))] + [whole] * nb
    args = [dense, *blocks]
    if acc is not None:
        specs.append(pl.BlockSpec((tm, 1024), lambda i: (start + i, 0)))
        args.append(acc)
    if add is not None:
        array, offset = add
        first = offset * BS // tm
        specs.append(pl.BlockSpec((tm, 1024), lambda i: (first + i, 0)))
        args.append(array)
    return pl.pallas_call(
        functools.partial(mm_kernel, nb, acc is not None, add is not None),
        out_shape=jax.ShapeDtypeStruct((count * tm, 1024), dtype),
        grid_spec=pltpu.PrefetchScalarGridSpec(
            num_scalar_prefetch=0,
            grid=(count,),
            in_specs=specs,
            out_specs=pl.BlockSpec((tm, 1024), lambda i: (i, 0)),
            scratch_shapes=[pltpu.VMEM((depth, 1024), jnp.bfloat16)],
        ),
        compiler_params=pltpu.CompilerParams(vmem_limit_bytes=VMEM),
        cost_estimate=pl.CostEstimate(
            flops=2 * count * tm * depth * 1024, transcendentals=0,
            bytes_accessed=count * tm * (depth * 2 + 1024 * 8) + depth * 2048),
    )(*args)


def join_weight_kernel(pos, mine_ref, other_ref, out_ref):
    _, _, zl, y, core, sign = place(pos)
    for other, ref in enumerate((mine_ref, other_ref)):
        for k in range(8):
            dy = (0, 3, 1, 2)[k // 2]
            owner = (zl ^ (k % 2)) * 8 + ((y + sign * (1 - 2 * other) * dy) & 3) * 2 + (core ^ other)
            at = pl.multiple_of(owner * 64, 64)
            out_ref[pl.ds(at, 64), :] = ref[k * 64:(k + 1) * 64, :]


def join_weight(pos, mine, other):
    return pl.pallas_call(
        join_weight_kernel,
        out_shape=jax.ShapeDtypeStruct((1024, 1024), jnp.bfloat16),
        grid_spec=pltpu.PrefetchScalarGridSpec(
            num_scalar_prefetch=1,
            grid=(1,),
            in_specs=[pl.BlockSpec((512, 1024), lambda i, pos: (0, 0))] * 2,
            out_specs=pl.BlockSpec((1024, 1024), lambda i, pos: (0, 0)),
        ),
        compiler_params=pltpu.CompilerParams(vmem_limit_bytes=VMEM),
        cost_estimate=pl.CostEstimate(flops=0, transcendentals=0, bytes_accessed=4 << 20),
        name="join_weight",
    )(pos, mine, other)


def last_kernel(a_ref, b_ref, c_ref, d_ref, w_ref, out_ref):
    total = a_ref[...].astype(jnp.float32) + b_ref[...].astype(jnp.float32)
    total = total + c_ref[...].astype(jnp.float32) + d_ref[...].astype(jnp.float32)
    product = jnp.dot(total.astype(jnp.bfloat16), w_ref[...], preferred_element_type=jnp.float32)
    out_ref[...] = jnp.maximum(product, 0.0).astype(out_ref.dtype)


def last(s0, f0, g0, far, weight):
    block = pl.BlockSpec((BS, 1024), lambda n: (0, 0))
    return pl.pallas_call(
        last_kernel,
        out_shape=jax.ShapeDtypeStruct((BS, 1024), jnp.bfloat16),
        grid=(1,),
        in_specs=[block, block, block, block, pl.BlockSpec((1024, 1024), lambda n: (0, 0))],
        out_specs=pl.BlockSpec((BS, 1024), lambda n: (0, 0)),
        compiler_params=pltpu.CompilerParams(vmem_limit_bytes=VMEM),
        cost_estimate=pl.CostEstimate(flops=2 * BS * 1024 * 1024, transcendentals=0, bytes_accessed=3 << 20),
        name="last",
    )(s0, f0, g0, far, weight)


def add32(*terms):
    total = terms[0].astype(jnp.float32)
    for term in terms[1:]:
        total = total + term.astype(jnp.float32)
    return total.astype(jnp.bfloat16)


def body(features, weight, tile_values, block_cols, tile_counts):
    perms = moves()

    def go(move, x):
        return lax.ppermute(x, ("row", "col"), perms[move])

    pos = jnp.stack([lax.axis_index("row"), lax.axis_index("col")]).astype(jnp.int32)

    b = {(0, 0): features}

    def block(z, x, move, source):
        b[z, x] = go(move, b[source])

    block(3, 0, "fz", (0, 0))
    block(1, 0, "gz", (0, 0))
    block(0, 3, "fx", (0, 0))
    block(0, 1, "gx", (0, 0))
    block(0, 2, "fx", (0, 3))
    block(2, 0, "fz", (3, 0))
    block(3, 3, "fx", (3, 0))
    block(3, 1, "gx", (3, 0))
    block(1, 3, "fx", (1, 0))
    block(1, 1, "gx", (1, 0))
    block(3, 2, "fz", (0, 2))
    block(1, 2, "gz", (0, 2))
    block(2, 3, "fx", (2, 0))
    block(2, 1, "gx", (2, 0))
    block(2, 2, "fx", (2, 3))
    in_order = [b[key] for key in K_ORDER]

    w2 = jnp.concatenate([weight, go("zl", weight)], axis=0)
    w3, w1 = go("fy", w2), go("gy", w2)
    w_mine = jnp.concatenate([w2, w3, w1, go("fy", w3)], axis=0)
    w_full = join_weight(pos, w_mine, go("core", w_mine))

    dense = dense_tile(pos, block_cols.reshape(128), tile_counts.reshape(16), tile_values[0, 0])
    acc = mm(dense, 0, in_order[:4], (0, 16), dtype=jnp.float32)
    acc = mm(dense, 4, in_order[4:8], (0, 16), acc=acc, dtype=jnp.float32)
    acc = mm(dense, 8, in_order[8:12], (0, 16), acc=acc, dtype=jnp.float32)
    tail = in_order[12:]

    def rows(start, count, add=None):
        return mm(dense, 12, tail, (start, count), acc=acc, add=add)

    send2 = rows(0, 2)
    got2 = go("core", send2)
    send31 = rows(2, 4)
    got31 = go("core", send31)
    s2 = rows(6, 2, (got2, 0))
    from2 = go("fy", s2)
    send0 = rows(8, 2)
    got0 = go("core", send0)
    s3 = rows(10, 2, (got31, 0))
    g0 = go("gy", s3)
    s1 = rows(12, 2, (got31, 2))
    s0 = rows(14, 2, (got0, 0))
    f0_far = go("fy", add32(s1[BS:], from2[BS:]))
    f0_near = go("fy", add32(s1[:BS], from2[:BS]))
    far = go("zl", add32(s0[BS:], g0[BS:], f0_far))
    return last(s0, g0, f0_near, far, w_full)


def solution(mesh):
    in_specs = (
        P(("col", "row"), None),
        P("col", None),
        P("row", "col", None, None, None, None),
        P("row", "col", None, None),
        P("row", "col", None),
    )
    out_specs = P(("row", "col"), None)
    return jax.shard_map(body, mesh=mesh, in_specs=in_specs, out_specs=out_specs, check_vma=False)
```
